32 devices in a mesh: gx: 4 (over y, core), gy: 2 (over x), gz: 4 (over z).
Axes of the slice: x: 2, y: 2, z: 4, core: 2. Of those that a mesh axis runs over, the one named last changes fastest.
Arguments:
- rhs: float32 [3, 64, 64, 512], P(None, 'gx', 'gy', 'gz'), may hold values from -6 to 6
- viscous: float32 [4, 4, 32], P('gx', 'gy', 'gz'), may hold values from 0.3 to 3
- reaction: float32 [4, 4, 32], P('gx', 'gy', 'gz'), may hold values from 0.05 to 1
Outputs:
- correction: float32 [3, 64, 64, 512], P(None, 'gx', 'gy', 'gz')
The draws below stay inside these ranges and needn't reach their ends.
All inputs are finite; a program needn't handle non-finite values.
Results may differ from the reference program's by a relative error of at most 0.00008.
Values sent between devices are 32-bit elements; how exact they have to be, the bound alone decides.
No kernel may reach another device: no remote copies, remote signals or barrier semaphores. Data moves between devices by JAX's collectives and lax.ppermute only.
A program may use at most 64 MiB of HBM per device.

```python
import math
import jax
import jax.numpy as jnp
from jax import lax

EDGE_POINTS = 16
COMP = 3
ELEMENTS_X = 4
ELEMENTS_Y = 4
ELEMENTS_Z = 32
NX = 64
NY = 64
NZ = 512


def levels(rng, extent, shards, smallest, high):
    gain = 1.0
    for dim, parts in shards:
        steps = jax.random.uniform(jax.random.fold_in(jax.random.fold_in(rng, 6), dim), (parts,), jnp.float32, smallest / len(shards), high / len(shards))
        gain = gain * jnp.repeat(jnp.exp(steps), extent[dim] // parts).reshape((-1,) + (1,) * (len(extent) - 1 - dim))
    return gain


def normal_values(key, extent, spread, limit, cuts=(), kind=jnp.bfloat16):
    drawn = spread * jax.random.normal(key, extent, jnp.float32)
    if cuts:
        drawn = drawn * levels(key, extent, cuts, -0.22, 0.18)
    return jnp.clip(drawn, -limit, limit).astype(kind)


def setup_inputs(seed: int = 0) -> dict:
    arg_keys = jax.random.split(jax.random.key(seed), 4)
    rhs = normal_values(arg_keys[0], (COMP, NX, NY, NZ), 1.0, 6.0, ((1, 4), (2, 2), (3, 4)), jnp.float32)
    viscous = jnp.clip(jnp.exp(math.log(3.0) - 2.3025851 * jax.random.uniform(arg_keys[1], (ELEMENTS_X, ELEMENTS_Y, ELEMENTS_Z), jnp.float32) ** levels(arg_keys[1], (ELEMENTS_X, ELEMENTS_Y, ELEMENTS_Z), ((0, 4), (1, 2), (2, 4)), -0.2, 0.2)), 0.3, 3.0)
    reaction = jnp.clip(jnp.exp(math.log(1.0) - 2.9957323 * jax.random.uniform(arg_keys[2], (ELEMENTS_X, ELEMENTS_Y, ELEMENTS_Z), jnp.float32) ** levels(arg_keys[2], (ELEMENTS_X, ELEMENTS_Y, ELEMENTS_Z), ((0, 4), (1, 2), (2, 4)), -0.2, 0.2)), 0.05, 1.0)
    return {"rhs": rhs, "viscous": viscous, "reaction": reaction}


highest = lax.Precision.HIGHEST

def tables():
    index = jnp.arange(EDGE_POINTS + 2).astype(jnp.float32)
    basis = jnp.sqrt(jnp.float32(2.0) / (EDGE_POINTS + 3)) * jnp.sin(jnp.pi * (index[:, None] + 1.0) * (index[None, :] + 1.0) / (EDGE_POINTS + 3))
    eigen_values = 2.0 - 2.0 * jnp.cos(jnp.pi * (index + 1.0) / (EDGE_POINTS + 3))
    return (basis, eigen_values)

def rear_part(values, axis, blocks):
    first_layer = lax.slice_in_dim(values, EDGE_POINTS, EDGE_POINTS * blocks + 1, stride=EDGE_POINTS, axis=axis)
    second_layer = lax.slice_in_dim(values, EDGE_POINTS + 1, EDGE_POINTS * blocks + 2, stride=EDGE_POINTS, axis=axis)
    return jnp.stack([first_layer, second_layer], axis=axis + 1)

def expand(field_values):
    spread_values = jnp.broadcast_to(field_values[:, None, :, None, :, None], (ELEMENTS_X, EDGE_POINTS, ELEMENTS_Y, EDGE_POINTS, ELEMENTS_Z, EDGE_POINTS))
    return spread_values.reshape(NX, NY, NZ)

def precondition(field, viscous, reaction):
    basis, eigen_values = tables()
    padded_field = jnp.pad(field, 1)
    span_along_x, span_along_y = (padded_field.shape[0], padded_field.shape[1])
    front_margin = padded_field[:, :, :EDGE_POINTS * ELEMENTS_Z].reshape(span_along_x, span_along_y, ELEMENTS_Z, EDGE_POINTS)
    rear_margin = rear_part(padded_field, 2, ELEMENTS_Z)
    eigen_modes = jnp.einsum('xyhp,pg->xyhg', front_margin, basis[:EDGE_POINTS], precision=highest) + jnp.einsum('xyhp,pg->xyhg', rear_margin, basis[EDGE_POINTS:], precision=highest)
    front_margin = eigen_modes[:, :EDGE_POINTS * ELEMENTS_Y].reshape(span_along_x, ELEMENTS_Y, EDGE_POINTS, ELEMENTS_Z, EDGE_POINTS + 2)
    rear_margin = rear_part(eigen_modes, 1, ELEMENTS_Y)
    eigen_modes = jnp.einsum('xfphg,pb->xfbhg', front_margin, basis[:EDGE_POINTS], precision=highest) + jnp.einsum('xfphg,pb->xfbhg', rear_margin, basis[EDGE_POINTS:], precision=highest)
    front_margin = eigen_modes[:EDGE_POINTS * ELEMENTS_X].reshape(ELEMENTS_X, EDGE_POINTS, ELEMENTS_Y, EDGE_POINTS + 2, ELEMENTS_Z, EDGE_POINTS + 2)
    rear_margin = rear_part(eigen_modes, 0, ELEMENTS_X)
    eigen_modes = jnp.einsum('epfbhg,pa->eafbhg', front_margin, basis[:EDGE_POINTS], precision=highest) + jnp.einsum('epfbhg,pa->eafbhg', rear_margin, basis[EDGE_POINTS:], precision=highest)
    lam_sum = eigen_values[:, None, None] + eigen_values[None, :, None] + eigen_values[None, None, :]
    divisor = viscous[:, None, :, None, :, None] * lam_sum[None, :, None, :, None, :] + reaction[:, None, :, None, :, None]
    eigen_modes = eigen_modes / divisor
    back_basis = basis[1:EDGE_POINTS + 1]
    local = jnp.einsum('eafbhg,qa->eqfbhg', eigen_modes, back_basis, precision=highest)
    local = jnp.einsum('eqfbhg,rb->eqfrhg', local, back_basis, precision=highest)
    local = jnp.einsum('eqfrhg,sg->eqfrhs', local, back_basis, precision=highest)
    return local.reshape(NX, NY, NZ)

def operate(field, viscous_pt, reaction_pt):
    padded_field = jnp.pad(field, 1)
    beside = padded_field[2:, 1:-1, 1:-1] + padded_field[:-2, 1:-1, 1:-1]
    beside = beside + padded_field[1:-1, 2:, 1:-1] + padded_field[1:-1, :-2, 1:-1]
    beside = beside + padded_field[1:-1, 1:-1, 2:] + padded_field[1:-1, 1:-1, :-2]
    return reaction_pt * field + viscous_pt * (6.0 * field - beside)

def reference(rhs, viscous, reaction):

    def single(field):
        first = precondition(field, viscous, reaction)
        residual = field - operate(first, expand(viscous), expand(reaction))
        return first + precondition(residual, viscous, reaction)
    return lax.map(single, rhs)
```

```python
import itertools

import jax
import jax.numpy as jnp
import numpy as np
from jax import lax
from jax.experimental import pallas as pl
from jax.experimental.pallas import tpu as pltpu
from jax.sharding import PartitionSpec as P

EDGE_POINTS = 16
WINDOW = EDGE_POINTS + 2
LANES = 128
ROWS = 336
PLANE = 384
AXES = ("gx", "gy", "gz")
f32, bf16 = jnp.float32, jnp.bfloat16


def pairings(n):
    if n == 1:
        return []
    even = [c ^ 1 if c ^ 1 < n else c for c in range(n)]
    if n == 2:
        return [even]
    odd = [(c + 1 if c % 2 else c - 1) for c in range(n)]
    odd = [t % n if n % 2 == 0 else (t if 0 <= t < n else c) for c, t in enumerate(odd)]
    return [even, odd]


def swap_pairs(sizes, maps):
    def linear(c):
        return (c[0] * sizes[1] + c[1]) * sizes[2] + c[2]

    return [
        (linear(c), linear(maps(c))) for c in itertools.product(*[range(k) for k in sizes])
    ]


def plan(sizes):
    tx, ty, tz = (pairings(k) for k in sizes)
    px = [swap_pairs(sizes, lambda c, t=t: (t[c[0]], c[1], c[2])) for t in tx]
    py = [swap_pairs(sizes, lambda c, t=t: (c[0], t[c[1]], c[2])) for t in ty]
    pxy = [
        swap_pairs(sizes, lambda c, t=t, s=s: (t[c[0]], s[c[1]], c[2])) for t in tx for s in ty
    ]
    pz = []
    for k, t in enumerate(tz):
        if k == 1 and sizes[2] % 2 == 0 and sizes[0] % 2 == 0:
            ends = (0, sizes[2] - 1)
            pz.append(
                swap_pairs(
                    sizes,
                    lambda c, t=t, ends=ends: (tx[0][c[0]], c[1], c[2])
                    if c[2] in ends
                    else (c[0], c[1], t[c[2]]),
                )
            )
        else:
            pz.append(swap_pairs(sizes, lambda c, t=t: (c[0], c[1], t[c[2]])))
    return px, py, pxy, pz


def window_order():
    inner = range(1, EDGE_POINTS + 1)
    last = EDGE_POINTS + 1
    order = [(i, j) for i in inner for j in inner]
    order += [(0, j) for j in inner] + [(last, j) for j in inner]
    order += [(i, 0) for i in inner] + [(i, last) for i in inner]
    return order + [(0, 0), (0, last), (last, 0), (last, last)]


def pieces(table):
    table = np.asarray(table, np.float32)
    lead = table.astype(jnp.bfloat16)
    return lead, (table - lead.astype(np.float32)).astype(jnp.bfloat16)


def tables(ey, ez, comps):
    index = np.arange(WINDOW)
    basis = np.sqrt(2.0 / (EDGE_POINTS + 3)) * np.sin(
        np.pi * (index[:, None] + 1.0) * (index[None, :] + 1.0) / (EDGE_POINTS + 3)
    )
    lam = 2.0 - 2.0 * np.cos(np.pi * (index + 1.0) / (EDGE_POINTS + 3))
    order = window_order()
    forward = np.zeros((ROWS, ROWS))
    for k, (i, j) in enumerate(order):
        forward[: WINDOW * WINDOW, k] = np.outer(basis[i], basis[j]).reshape(-1)
    inner = basis[1 : EDGE_POINTS + 1]
    back = np.zeros((EDGE_POINTS * EDGE_POINTS, ROWS))
    back[:, : WINDOW * WINDOW] = np.kron(inner, inner)
    lam_xy = np.ones((ROWS, 1), np.float32)
    lam_xy[: WINDOW * WINDOW, 0] = (lam[:, None] + lam[None, :]).reshape(-1)
    nz, width = EDGE_POINTS * ez, WINDOW * ez
    depth = np.zeros((nz + 2, 2 * LANES))
    depth_back = np.zeros((2 * LANES, nz))
    lam_z = np.zeros((1, 2 * LANES), np.float32)
    for h in range(ez):
        cols = slice(h * WINDOW, (h + 1) * WINDOW)
        depth[h * EDGE_POINTS : h * EDGE_POINTS + WINDOW, cols] = basis
        depth_back[cols, h * EDGE_POINTS : (h + 1) * EDGE_POINTS] = inner.T
        lam_z[0, cols] = lam
    fh, fl = pieces(forward)
    bh, bl = pieces(back)
    zh, zl = pieces(depth)
    ih, il = pieces(depth_back)
    ahead = np.concatenate([fh, fh, fl], axis=1)
    behind = np.concatenate([bh, bh, bl], axis=1)
    core = slice(1, nz + 1)
    z_ahead = np.concatenate([zh[core], zh[core], zl[core]], axis=0)
    rim = [0, nz + 1, 1, nz]
    z_rim = np.zeros((ey * comps, LANES, 2 * LANES), jnp.bfloat16)
    part = ey * 16
    for f in range(ey):
        for c in range(comps):
            for r, row in enumerate(rim):
                lane = f * 16 + 4 * c + r
                z_rim[f * comps + c, lane] = zh[row]
                z_rim[f * comps + c, part + lane] = zh[row]
                z_rim[f * comps + c, 2 * part + lane] = zl[row]
    tail = np.zeros((LANES, nz), jnp.bfloat16)
    rest = width - LANES
    for k, piece in enumerate((ih, ih, il)):
        tail[k * 32 : k * 32 + rest] = piece[LANES:width]
    z_behind = np.concatenate([ih[:LANES], ih[:LANES], il[:LANES], tail], axis=0)
    return ahead, behind, z_ahead, z_rim, z_behind, lam_xy, lam_z


def split(v):
    lead = v.astype(bf16)
    return lead, (v - lead.astype(f32)).astype(bf16)


def three(v):
    lead, rest = split(v)
    return lead, rest, lead


def both_sides(position, count, arrays):
    if not arrays:
        return None, None
    if len(arrays) == 1:
        low = high = arrays[0]
    else:
        odd = position % 2 == 1
        low = jnp.where(odd, arrays[0], arrays[1])
        high = jnp.where(odd, arrays[1], arrays[0])
    return (
        jnp.where(position > 0, low, jnp.zeros_like(low)),
        jnp.where(position < count - 1, high, jnp.zeros_like(high)),
    )


def four_corners(at, sizes, arrays, ny_types):
    rows = [arrays[k : k + ny_types] for k in range(0, len(arrays), ny_types)]
    by_y = [both_sides(at[0], sizes[0], [r[t] for r in rows]) for t in range(ny_types)]
    return [both_sides(at[1], sizes[1], [b[side] for b in by_y]) for side in (0, 1)]


def ends(position, kind, first, last):
    even = position % 2 == (1 if kind else 0)
    return jnp.where(even, last, first)


def lane_row(ref, f, ez, step, width, fill=0.0):
    lane = lax.broadcasted_iota(jnp.int32, (1, width), 1)
    row = jnp.full((1, width), fill, f32)
    for h in range(ez):
        row = jnp.where((lane >= h * step) & (lane < (h + 1) * step), ref[0, f, h], row)
    return row


def pack_sides(at, fields, outs, counts, extra=None):
    tx, ty = counts
    nx, ny = fields[0][0].shape[1], fields[0][0].shape[2]
    x_outs, y_outs, xy_outs = outs[:tx], outs[tx : tx + ty], outs[tx + ty :]
    total = len(fields)
    for m, (ref, c) in enumerate(fields):
        for k in range(tx):
            x_outs[k][m * ny : (m + 1) * ny, :] = ends(at[0], k, ref[c, 0], ref[c, nx - 1])
        if ty:
            low, high = ref[c, :, 0, :], ref[c, :, ny - 1, :]
        for k in range(ty):
            y_outs[k][m * nx : (m + 1) * nx, :] = ends(at[1], k, low, high)
        for k in range(tx):
            for s in range(ty):
                near = ends(at[1], s, ref[c, 0, 0:1, :], ref[c, 0, ny - 1 : ny, :])
                far = ends(at[1], s, ref[c, nx - 1, 0:1, :], ref[c, nx - 1, ny - 1 : ny, :])
                xy_outs[k * ty + s][m : m + 1, :] = ends(at[0], k, near, far)
    if extra is not None:
        ey = len(extra)
        for k in range(tx):
            for f in range(ey):
                x_outs[k][total * ny + f : total * ny + f + 1, :] = extra[f]
        for k in range(ty):
            y_outs[k][total * nx : total * nx + 1, :] = ends(at[1], k, extra[0], extra[-1])
        for k in range(tx):
            for s in range(ty):
                xy_outs[k * ty + s][total : total + 1, :] = ends(at[1], s, extra[0], extra[-1])


def fill_window(out, k, f, ey, core, strip, xb, xa, yb, ya, corner):
    e = EDGE_POINTS
    for x in range(e):
        out[k, x * e : (x + 1) * e, :] = core(x, f)
    at = e * e
    out[k, at : at + e, :] = xb[f * e : (f + 1) * e]
    out[k, at + e : at + 2 * e, :] = xa[f * e : (f + 1) * e]
    out[k, at + 2 * e : at + 3 * e, :] = yb if f == 0 else strip(f * e - 1)
    out[k, at + 3 * e : at + 4 * e, :] = ya if f == ey - 1 else strip((f + 1) * e)
    at += 4 * e
    out[k, at : at + e, :] = jnp.zeros((e, LANES), f32)
    for s, face in enumerate((xb, xa)):
        low = corner[s][0] if f == 0 else face[f * e - 1 : f * e]
        high = corner[s][1] if f == ey - 1 else face[(f + 1) * e : (f + 1) * e + 1]
        out[k, at + 2 * s : at + 2 * s + 1, :] = low
        out[k, at + 2 * s + 1 : at + 2 * s + 2, :] = high


def gather_columns(columns, refs):
    lane = lax.broadcasted_iota(jnp.int32, (ROWS, LANES), 1)
    total = jnp.zeros((ROWS, LANES), f32)
    for to, ref, k in refs:
        turned = pltpu.roll(ref[k], to + 1, axis=1)
        total = jnp.where((lane == to) | (lane == to + 1), turned, total)
    columns[0:ROWS, :] = total
    columns[ROWS:PLANE, :] = jnp.zeros((PLANE - ROWS, LANES), f32)


def solution(mesh):
    sizes = tuple(mesh.shape[a] for a in AXES)
    px, py, pxy, pz = plan(sizes)
    tx, ty, tz = len(px), len(py), len(pz)

    def here():
        return [lax.axis_index(a) for a in AXES]

    def shards(rhs, viscous, reaction):
        comps, nx, ny, nz = rhs.shape
        ex, ey, ez = viscous.shape
        e = EDGE_POINTS
        assert ex == 1 and nz == LANES and WINDOW * ez <= 160 and ey * 48 <= LANES and comps <= 3
        consts = [jnp.asarray(t) for t in tables(ey, ez, comps)]
        ahead, behind, z_ahead, z_rim, z_behind, lam_xy, lam_z = consts
        many = ey * comps
        vmem = pl.BlockSpec(memory_space=pltpu.VMEM)
        smem = pl.BlockSpec(memory_space=pltpu.SMEM)

        def shape(*dims, dtype=f32):
            return jax.ShapeDtypeStruct(dims, dtype)

        def call(kernel, outs, args, scratch=(), smems=0, name=None, flops=0):
            return pl.pallas_call(
                kernel,
                out_shape=outs,
                in_specs=[smem] * smems + [vmem] * (len(args) - smems),
                out_specs=[vmem] * len(outs),
                scratch_shapes=list(scratch),
                name=name,
            )(*args)

        def side_shapes(fields, more):
            return (
                [shape(fields * ny + more, nz)] * tx
                + [shape(fields * nx + more, nz)] * ty
                + [shape(8, nz)] * (tx * ty)
            )

        def send(arrays):
            out = []
            for a, pairs in zip(arrays, px + py + pxy):
                out.append(lax.ppermute(a, AXES, pairs))
            return out

        def received(at, refs, fields, with_extra):
            xs = both_sides(at[0], sizes[0], [r[...] for r in refs[:tx]])
            ys = both_sides(at[1], sizes[1], [r[...] for r in refs[tx : tx + ty]])
            if tx and ty:
                cs = four_corners(at, sizes, [r[...] for r in refs[tx + ty :]], ty)
            else:
                cs = [[jnp.zeros((8, nz), f32)] * 2] * 2
            more = 8 if with_extra else 0
            xs = [v if v is not None else jnp.zeros((fields * ny + more, nz), f32) for v in xs]
            ys = [v if v is not None else jnp.zeros((fields * nx + more, nz), f32) for v in ys]
            return xs, ys, cs

        def pack_kernel(vis, field, *outs):
            at = here()
            rows = [lane_row(vis, f, ez, e, nz) for f in range(ey)]
            pack_sides(at, [(field, c) for c in range(comps)], outs, (tx, ty), rows)

        faces = call(
            pack_kernel, side_shapes(comps, 8), [viscous, rhs], smems=1, name="pack_faces"
        )
        faces = send(faces)

        def window_kernel(vis, field, *refs):
            at = here()
            sides, (win, cols_out, around, coef, columns) = refs[:-5], refs[-5:]
            xs, ys, cs = received(at, sides, comps, True)
            pick = lambda v, c, n: v[c * n : (c + 1) * n]
            for c in range(comps):
                for f in range(ey):
                    fill_window(
                        win,
                        f * comps + c,
                        f,
                        ey,
                        lambda x, f: field[c, x, f * e : (f + 1) * e, :],
                        lambda y: field[c, :, y, :],
                        pick(xs[0], c, ny),
                        pick(xs[1], c, ny),
                        pick(ys[0], c, nx),
                        pick(ys[1], c, nx),
                        [[cs[s][t][c : c + 1] for t in (0, 1)] for s in (0, 1)],
                    )
            own = [lane_row(vis, f, ez, e, nz) for f in range(ey)]
            vx = [[xs[s][comps * ny + f : comps * ny + f + 1] for f in range(ey)] for s in (0, 1)]
            vy = [ys[s][comps * nx : comps * nx + 1] for s in (0, 1)]
            vc = [[cs[s][t][comps : comps + 1] for t in (0, 1)] for s in (0, 1)]
            flat = vx[0] + vx[1] + vy + vc[0] + vc[1]
            for k, row in enumerate(flat):
                around[k : k + 1, :] = row
            wide = lambda row: jnp.broadcast_to(row, (e, nz))
            for f in range(ey):
                face = [jnp.concatenate([wide(v) for v in vx[s]], axis=0) for s in (0, 1)]
                fill_window(
                    coef,
                    f,
                    f,
                    ey,
                    lambda x, f: wide(own[f]),
                    lambda y: wide(own[y // e]),
                    face[0],
                    face[1],
                    wide(vy[0]),
                    wide(vy[1]),
                    vc,
                )
            entries = []
            for f in range(ey):
                entries += [(f * 8 + 2 * c, win, f * comps + c) for c in range(comps)]
                entries += [(f * 8 + 2 * comps, coef, f)]
            gather_columns(columns, entries)
            cols_out[...] = columns[...].T[: ey * 8]

        windows, columns, around = call(
            window_kernel,
            [shape(many, ROWS, nz), shape(ey * 8, PLANE), shape(16, nz)],
            [viscous, rhs] + faces,
            [pltpu.VMEM((ey, ROWS, nz), f32), pltpu.VMEM((PLANE, LANES), f32)],
            smems=1,
            name="windows",
        )

        def send_z(array):
            return [lax.ppermute(array, AXES, pairs) for pairs in pz]

        def forward_kernel(win, ahead, z_ahead, out, stacked, mixed):
            for k in range(many):
                for p, piece in enumerate(three(win[k])):
                    stacked[p * ROWS : (p + 1) * ROWS, k * nz : (k + 1) * nz] = piece
            mixed[...] = jnp.dot(ahead[...], stacked[...], preferred_element_type=f32)
            for k in range(many):
                wide = jnp.concatenate(three(mixed[:, k * nz : (k + 1) * nz]), axis=1)
                out[k] = jnp.dot(wide, z_ahead[...], preferred_element_type=f32)

        def forward(windows):
            return call(
                forward_kernel,
                [shape(many, ROWS, 2 * LANES)],
                [windows, ahead, z_ahead],
                [pltpu.VMEM((3 * ROWS, many * nz), bf16), pltpu.VMEM((ROWS, many * nz), f32)],
                name="forward",
            )[0]

        def finish(store, modes, rim, tabs, vis, rea, stacked_rim, stacked):
            ahead, behind, z_rim, z_behind, lam_xy, lam_z = tabs
            lane = lax.broadcasted_iota(jnp.int32, (ROWS, LANES), 1)
            turned = rim[...].T
            for p, piece in enumerate(three(turned[:ROWS])):
                stacked_rim[p * ROWS : (p + 1) * ROWS, :] = piece
            plane = jnp.dot(ahead[...], stacked_rim[...], preferred_element_type=f32)

            def beside(v, part):
                lead, rest = split(v)
                lead, rest = lead.astype(f32), rest.astype(f32)
                both = jnp.where(lane < part, lead, pltpu.roll(rest, part, axis=1))
                far = jnp.where(lane < 2 * part, both, pltpu.roll(lead, 2 * part, axis=1))
                return far.astype(bf16)

            plane = beside(plane, ey * 16)
            for f in range(ey):
                v = lane_row(vis, f, ez, WINDOW, 2 * LANES)
                r = lane_row(rea, f, ez, WINDOW, 2 * LANES, fill=1.0)
                scale = 1.0 / (v * (lam_xy[...] + lam_z[...]) + r)
                for c in range(comps):
                    k = f * comps + c
                    m = modes[k] + jnp.dot(plane, z_rim[k], preferred_element_type=f32)
                    m = m * scale
                    lead, rest = split(m[:, :LANES])
                    tail = beside(m[:, LANES:], 32)
                    wide = jnp.concatenate([lead, rest, lead, tail], axis=1)
                    back = jnp.dot(wide, z_behind[...], preferred_element_type=f32)
                    for p, piece in enumerate(three(back)):
                        stacked[p * ROWS : (p + 1) * ROWS, k * nz : (k + 1) * nz] = piece
            local = jnp.dot(behind[...], stacked[...], preferred_element_type=f32)
            for f in range(ey):
                for c in range(comps):
                    k = f * comps + c
                    for x in range(nx):
                        store(c, x, f, local[x * e : (x + 1) * e, k * nz : (k + 1) * nz])

        tabs = [ahead, behind, z_rim, z_behind, lam_xy, lam_z]
        finish_scratch = [
            pltpu.VMEM((LANES, PLANE), f32),
            pltpu.VMEM((3 * ROWS, LANES), bf16),
            pltpu.VMEM((3 * ROWS, many * nz), bf16),
        ]

        def z_sides(at, refs, rows):
            got = both_sides(at[2], sizes[2], [r[...] for r in refs])
            return [v if v is not None else jnp.zeros((rows, PLANE), f32) for v in got]

        def first_kernel(vis, rea, field, modes, *refs):
            at = here()
            zs, refs = refs[:tz], refs[tz:]
            tabs, refs = refs[:6], refs[6:]
            first, part = refs[:2]
            outs, (rim, stacked_rim, stacked) = refs[2:-3], refs[-3:]
            low, high = z_sides(at, zs, ey * 8)
            rim[...] = jnp.zeros((LANES, PLANE), f32)
            for f in range(ey):
                for c in range(comps):
                    to, src = f * 16 + 4 * c, f * 8 + 2 * c
                    rim[to : to + 1, :] = low[src : src + 1]
                    rim[to + 1 : to + 2, :] = high[src + 1 : src + 2]

            def store(c, x, f, rows):
                first[c, x, f * e : (f + 1) * e, :] = rows

            finish(store, modes, rim, tabs, vis, rea, stacked_rim, stacked)
            wide = lambda row: jnp.broadcast_to(row, (e, nz))
            v = jnp.concatenate([wide(lane_row(vis, f, ez, e, nz)) for f in range(ey)], axis=0)
            r = jnp.concatenate([wide(lane_row(rea, f, ez, e, nz)) for f in range(ey)], axis=0)
            row = lax.broadcasted_iota(jnp.int32, (ny, nz), 0)
            lane = lax.broadcasted_iota(jnp.int32, (ny, nz), 1)
            for c in range(comps):
                for x in range(nx):
                    u = first[c, x]
                    near = jnp.where(row > 0, pltpu.roll(u, 1, axis=0), 0.0)
                    near += jnp.where(row < ny - 1, pltpu.roll(u, ny - 1, axis=0), 0.0)
                    near += jnp.where(lane > 0, pltpu.roll(u, 1, axis=1), 0.0)
                    near += jnp.where(lane < nz - 1, pltpu.roll(u, nz - 1, axis=1), 0.0)
                    if x > 0:
                        near += first[c, x - 1]
                    if x < nx - 1:
                        near += first[c, x + 1]
                    part[c, x] = field[c, x] - (r * u + v * (6.0 * u - near))
            fields = [(first, c) for c in range(comps)] + [(part, c) for c in range(comps)]
            pack_sides(at, fields, outs, (tx, ty))

        def residual_kernel(vis, first, part, around, *refs):
            at = here()
            sides, (win, cols_out, whole, own, columns) = refs[:-5], refs[-5:]
            xs, ys, cs = received(at, sides, 2 * comps, False)
            row = lax.broadcasted_iota(jnp.int32, (ny, nz), 0)
            line = lax.broadcasted_iota(jnp.int32, (nx, nz), 0)
            wide = lambda r: jnp.broadcast_to(r, (e, nz))
            mine = [lane_row(vis, f, ez, e, nz) for f in range(ey)]
            v = jnp.concatenate([wide(m) for m in mine], axis=0)
            near = lambda k: around[k : k + 1, :]
            vx = [
                jnp.concatenate([wide(near(s * ey + f)) for f in range(ey)], axis=0)
                for s in (0, 1)
            ]
            vy = [near(2 * ey + s) for s in (0, 1)]
            vc = [[near(2 * ey + 2 + 2 * s + t) for t in (0, 1)] for s in (0, 1)]
            for c in range(comps):
                ux = [xs[s][c * ny : (c + 1) * ny] for s in (0, 1)]
                rx = [xs[s][(comps + c) * ny : (comps + c + 1) * ny] for s in (0, 1)]
                uy = [ys[s][c * nx : (c + 1) * nx] for s in (0, 1)]
                ry = [ys[s][(comps + c) * nx : (comps + c + 1) * nx] for s in (0, 1)]
                uc = [[cs[s][t][c : c + 1] for t in (0, 1)] for s in (0, 1)]
                rc = [[cs[s][t][comps + c : comps + c + 1] for t in (0, 1)] for s in (0, 1)]
                at_x = (0, nx - 1)
                at_y = (0, ny - 1)
                for x in range(nx):
                    value = part[c, x]
                    for s in (0, 1):
                        if x == at_x[s]:
                            value += v * ux[s]
                    whole[x] = value
                for s in (0, 1):
                    f = 0 if s == 0 else ey - 1
                    whole[:, at_y[s], :] = whole[:, at_y[s], :] + mine[f] * uy[s]
                face_x = []
                for s in (0, 1):
                    beyond = jnp.where(row == 0, uc[s][0], jnp.where(row == ny - 1, uc[s][1], 0.0))
                    face_x.append(rx[s] + vx[s] * (first[c, at_x[s]] + beyond))
                face_y = []
                for t in (0, 1):
                    beyond = jnp.where(
                        line == 0, uc[0][t], jnp.where(line == nx - 1, uc[1][t], 0.0)
                    )
                    face_y.append(ry[t] + vy[t] * (first[c, :, at_y[t], :] + beyond))
                corner = [
                    [
                        rc[s][t]
                        + vc[s][t]
                        * (
                            ux[s][at_y[t] : at_y[t] + 1]
                            + uy[t][at_x[s] : at_x[s] + 1]
                        )
                        for t in (0, 1)
                    ]
                    for s in (0, 1)
                ]
                for f in range(ey):
                    k = f * comps + c
                    fill_window(
                        win,
                        k,
                        f,
                        ey,
                        lambda x, f: whole[x, f * e : (f + 1) * e, :],
                        lambda y: whole[:, y, :],
                        face_x[0],
                        face_x[1],
                        face_y[0],
                        face_y[1],
                        corner,
                    )
                    fill_window(
                        own,
                        k,
                        f,
                        ey,
                        lambda x, f: first[c, x, f * e : (f + 1) * e, :],
                        lambda y: first[c, :, y, :],
                        ux[0],
                        ux[1],
                        uy[0],
                        uy[1],
                        uc,
                    )
            entries = []
            for f in range(ey):
                for c in range(comps):
                    k = f * comps + c
                    entries.append((f * 16 + 2 * c, own, k))
                    entries.append((f * 16 + 2 * (comps + c), win, k))
            gather_columns(columns, entries)
            cols_out[...] = columns[...].T[: ey * 16]

        def last_kernel(vis, rea, first, modes, mine, coef, *refs):
            at = here()
            coefs, zs, refs = refs[:tz], refs[tz : 2 * tz], refs[2 * tz :]
            tabs, (out, rim, stacked_rim, stacked) = refs[:6], refs[6:]
            low, high = z_sides(at, zs, ey * 16)
            vlow, vhigh = z_sides(at, coefs, ey * 8)
            rim[...] = jnp.zeros((LANES, PLANE), f32)
            for f in range(ey):
                cv = f * 8 + 2 * comps
                v_last, v_first = coef[cv : cv + 1, :], coef[cv + 1 : cv + 2, :]
                for c in range(comps):
                    to, u, r = f * 16 + 4 * c, f * 16 + 2 * c, f * 16 + 2 * (comps + c)
                    u_last, u_first = mine[u : u + 1, :], mine[u + 1 : u + 2, :]
                    rim[to : to + 1, :] = low[r : r + 1] + vlow[cv : cv + 1] * u_first
                    rim[to + 1 : to + 2, :] = (
                        high[r + 1 : r + 2] + vhigh[cv + 1 : cv + 2] * u_last
                    )
                    rim[to + 2 : to + 3, :] = v_first * low[u : u + 1]
                    rim[to + 3 : to + 4, :] = v_last * high[u + 1 : u + 2]

            def store(c, x, f, rows):
                here_rows = slice(f * e, (f + 1) * e)
                out[c, x, here_rows, :] = first[c, x, here_rows, :] + rows

            finish(store, modes, rim, tabs, vis, rea, stacked_rim, stacked)

        z_first = send_z(columns)
        modes = forward(windows)
        results = call(
            first_kernel,
            [shape(*rhs.shape), shape(*rhs.shape)] + side_shapes(2 * comps, 0),
            [viscous, reaction, rhs, modes] + z_first + tabs,
            finish_scratch,
            smems=2,
            name="first",
        )
        first, part = results[:2]
        faces = send(results[2:])
        windows, columns2 = call(
            residual_kernel,
            [shape(many, ROWS, nz), shape(ey * 16, PLANE)],
            [viscous, first, part, around] + faces,
            [
                pltpu.VMEM((nx, ny, nz), f32),
                pltpu.VMEM((many, ROWS, nz), f32),
                pltpu.VMEM((PLANE, LANES), f32),
            ],
            smems=1,
            name="residual",
        )
        z_second = send_z(columns2)
        modes = forward(windows)
        return call(
            last_kernel,
            [shape(*rhs.shape)],
            [viscous, reaction, first, modes, columns2, columns] + z_first + z_second + tabs,
            finish_scratch,
            smems=2,
            name="last",
        )[0]

    placed = (P(None, *AXES), P(*AXES), P(*AXES))
    return jax.shard_map(
        shards, mesh=mesh, in_specs=placed, out_specs=P(None, *AXES), check_vma=False
    )
```

```python
import itertools

import jax
import jax.numpy as jnp
import numpy as np
from jax import lax
from jax.experimental import pallas as pl
from jax.experimental.pallas import tpu as pltpu
from jax.sharding import PartitionSpec as P

EDGE_POINTS = 16
WINDOW = EDGE_POINTS + 2
LANES = 128
ROWS = 336
PLANE = 384
AXES = ("gx", "gy", "gz")
f32, bf16 = jnp.float32, jnp.bfloat16


def pairings(n):
    if n == 1:
        return []
    even = [c ^ 1 if c ^ 1 < n else c for c in range(n)]
    if n == 2:
        return [even]
    odd = [(c + 1 if c % 2 else c - 1) for c in range(n)]
    odd = [t % n if n % 2 == 0 else (t if 0 <= t < n else c) for c, t in enumerate(odd)]
    return [even, odd]


def swap_pairs(sizes, maps):
    def linear(c):
        return (c[0] * sizes[1] + c[1]) * sizes[2] + c[2]

    return [
        (linear(c), linear(maps(c))) for c in itertools.product(*[range(k) for k in sizes])
    ]


def plan(sizes):
    tx, ty, tz = (pairings(k) for k in sizes)
    px = [swap_pairs(sizes, lambda c, t=t: (t[c[0]], c[1], c[2])) for t in tx]
    py = [swap_pairs(sizes, lambda c, t=t: (c[0], t[c[1]], c[2])) for t in ty]
    pxy = [
        swap_pairs(sizes, lambda c, t=t, s=s: (t[c[0]], s[c[1]], c[2])) for t in tx for s in ty
    ]
    pz = []
    for k, t in enumerate(tz):
        if k == 1 and sizes[2] % 2 == 0 and sizes[0] % 2 == 0:
            ends = (0, sizes[2] - 1)
            pz.append(
                swap_pairs(
                    sizes,
                    lambda c, t=t, ends=ends: (tx[0][c[0]], c[1], c[2])
                    if c[2] in ends
                    else (c[0], c[1], t[c[2]]),
                )
            )
        else:
            pz.append(swap_pairs(sizes, lambda c, t=t: (c[0], c[1], t[c[2]])))
    return px, py, pxy, pz


def window_order():
    inner = range(1, EDGE_POINTS + 1)
    last = EDGE_POINTS + 1
    order = [(i, j) for i in inner for j in inner]
    order += [(0, j) for j in inner] + [(last, j) for j in inner]
    order += [(i, 0) for i in inner] + [(i, last) for i in inner]
    return order + [(0, 0), (0, last), (last, 0), (last, last)]


def pieces(table):
    table = np.asarray(table, np.float32)
    lead = table.astype(jnp.bfloat16)
    return lead, (table - lead.astype(np.float32)).astype(jnp.bfloat16)


def tables(ey, ez, comps):
    index = np.arange(WINDOW)
    basis = np.sqrt(2.0 / (EDGE_POINTS + 3)) * np.sin(
        np.pi * (index[:, None] + 1.0) * (index[None, :] + 1.0) / (EDGE_POINTS + 3)
    )
    lam = 2.0 - 2.0 * np.cos(np.pi * (index + 1.0) / (EDGE_POINTS + 3))
    order = window_order()
    forward = np.zeros((ROWS, ROWS))
    for k, (i, j) in enumerate(order):
        forward[: WINDOW * WINDOW, k] = np.outer(basis[i], basis[j]).reshape(-1)
    inner = basis[1 : EDGE_POINTS + 1]
    back = np.zeros((EDGE_POINTS * EDGE_POINTS, ROWS))
    back[:, : WINDOW * WINDOW] = np.kron(inner, inner)
    lam_xy = np.ones((ROWS, 1), np.float32)
    lam_xy[: WINDOW * WINDOW, 0] = (lam[:, None] + lam[None, :]).reshape(-1)
    nz, width = EDGE_POINTS * ez, WINDOW * ez
    depth = np.zeros((nz + 2, 2 * LANES))
    depth_back = np.zeros((2 * LANES, nz))
    lam_z = np.zeros((1, 2 * LANES), np.float32)
    for h in range(ez):
        cols = slice(h * WINDOW, (h + 1) * WINDOW)
        depth[h * EDGE_POINTS : h * EDGE_POINTS + WINDOW, cols] = basis
        depth_back[cols, h * EDGE_POINTS : (h + 1) * EDGE_POINTS] = inner.T
        lam_z[0, cols] = lam
    fh, fl = pieces(forward)
    bh, bl = pieces(back)
    zh, zl = pieces(depth)
    ih, il = pieces(depth_back)
    ahead = np.concatenate([fh, fh, fl], axis=1)
    behind = np.concatenate([bh, bh, bl], axis=1)
    core = slice(1, nz + 1)
    z_ahead = np.concatenate([zh[core], zh[core], zl[core]], axis=0)
    rim = [0, nz + 1, 1, nz]
    z_rim = np.zeros((ey * comps, LANES, 2 * LANES), jnp.bfloat16)
    part = ey * 16
    for f in range(ey):
        for c in range(comps):
            for r, row in enumerate(rim):
                lane = f * 16 + 4 * c + r
                z_rim[f * comps + c, lane] = zh[row]
                z_rim[f * comps + c, part + lane] = zh[row]
                z_rim[f * comps + c, 2 * part + lane] = zl[row]
    tail = np.zeros((LANES, nz), jnp.bfloat16)
    rest = width - LANES
    for k, piece in enumerate((ih, ih, il)):
        tail[k * 32 : k * 32 + rest] = piece[LANES:width]
    z_behind = np.concatenate([ih[:LANES], ih[:LANES], il[:LANES], tail], axis=0)
    return ahead, behind, z_ahead, z_rim, z_behind, lam_xy, lam_z


def split(v):
    lead = v.astype(bf16)
    return lead, (v - lead.astype(f32)).astype(bf16)


def three(v):
    lead, rest = split(v)
    return lead, rest, lead


def both_sides(position, count, arrays):
    if not arrays:
        return None, None
    if len(arrays) == 1:
        low = high = arrays[0]
    else:
        odd = position % 2 == 1
        low = jnp.where(odd, arrays[0], arrays[1])
        high = jnp.where(odd, arrays[1], arrays[0])
    return (
        jnp.where(position > 0, low, jnp.zeros_like(low)),
        jnp.where(position < count - 1, high, jnp.zeros_like(high)),
    )


def four_corners(at, sizes, arrays, ny_types):
    rows = [arrays[k : k + ny_types] for k in range(0, len(arrays), ny_types)]
    by_y = [both_sides(at[0], sizes[0], [r[t] for r in rows]) for t in range(ny_types)]
    return [both_sides(at[1], sizes[1], [b[side] for b in by_y]) for side in (0, 1)]


def ends(position, kind, first, last):
    even = position % 2 == (1 if kind else 0)
    return jnp.where(even, last, first)


def lane_row(ref, f, ez, step, width, fill=0.0):
    lane = lax.broadcasted_iota(jnp.int32, (1, width), 1)
    row = jnp.full((1, width), fill, f32)
    for h in range(ez):
        row = jnp.where((lane >= h * step) & (lane < (h + 1) * step), ref[0, f, h], row)
    return row


def pack_sides(at, fields, outs, counts, extra=None):
    tx, ty = counts
    nx, ny = fields[0][0].shape[1], fields[0][0].shape[2]
    x_outs, y_outs, xy_outs = outs[:tx], outs[tx : tx + ty], outs[tx + ty :]
    total = len(fields)
    for m, (ref, c) in enumerate(fields):
        for k in range(tx):
            x_outs[k][m * ny : (m + 1) * ny, :] = ends(at[0], k, ref[c, 0], ref[c, nx - 1])
        if ty:
            low, high = ref[c, :, 0, :], ref[c, :, ny - 1, :]
        for k in range(ty):
            y_outs[k][m * nx : (m + 1) * nx, :] = ends(at[1], k, low, high)
        for k in range(tx):
            for s in range(ty):
                near = ends(at[1], s, ref[c, 0, 0:1, :], ref[c, 0, ny - 1 : ny, :])
                far = ends(at[1], s, ref[c, nx - 1, 0:1, :], ref[c, nx - 1, ny - 1 : ny, :])
                xy_outs[k * ty + s][m : m + 1, :] = ends(at[0], k, near, far)
    if extra is not None:
        ey = len(extra)
        for k in range(tx):
            for f in range(ey):
                x_outs[k][total * ny + f : total * ny + f + 1, :] = extra[f]
        for k in range(ty):
            y_outs[k][total * nx : total * nx + 1, :] = ends(at[1], k, extra[0], extra[-1])
        for k in range(tx):
            for s in range(ty):
                xy_outs[k * ty + s][total : total + 1, :] = ends(at[1], s, extra[0], extra[-1])


def fill_window(out, k, f, ey, core, strip, xb, xa, yb, ya, corner):
    e = EDGE_POINTS
    for x in range(e):
        out[k, x * e : (x + 1) * e, :] = core(x, f)
    at = e * e
    out[k, at : at + e, :] = xb[f * e : (f + 1) * e]
    out[k, at + e : at + 2 * e, :] = xa[f * e : (f + 1) * e]
    out[k, at + 2 * e : at + 3 * e, :] = yb if f == 0 else strip(f * e - 1)
    out[k, at + 3 * e : at + 4 * e, :] = ya if f == ey - 1 else strip((f + 1) * e)
    at += 4 * e
    out[k, at : at + e, :] = jnp.zeros((e, LANES), f32)
    for s, face in enumerate((xb, xa)):
        low = corner[s][0] if f == 0 else face[f * e - 1 : f * e]
        high = corner[s][1] if f == ey - 1 else face[(f + 1) * e : (f + 1) * e + 1]
        out[k, at + 2 * s : at + 2 * s + 1, :] = low
        out[k, at + 2 * s + 1 : at + 2 * s + 2, :] = high


def gather_columns(columns, refs):
    lane = lax.broadcasted_iota(jnp.int32, (ROWS, LANES), 1)
    total = jnp.zeros((ROWS, LANES), f32)
    for to, ref, k in refs:
        turned = pltpu.roll(ref[k], to + 1, axis=1)
        total = jnp.where((lane == to) | (lane == to + 1), turned, total)
    columns[0:ROWS, :] = total
    columns[ROWS:PLANE, :] = jnp.zeros((PLANE - ROWS, LANES), f32)


def solution(mesh):
    sizes = tuple(mesh.shape[a] for a in AXES)
    px, py, pxy, pz = plan(sizes)
    tx, ty, tz = len(px), len(py), len(pz)

    def here():
        return [lax.axis_index(a) for a in AXES]

    def shards(rhs, viscous, reaction):
        comps, nx, ny, nz = rhs.shape
        ex, ey, ez = viscous.shape
        e = EDGE_POINTS
        assert ex == 1 and nz == LANES and WINDOW * ez <= 160 and ey * 48 <= LANES and comps <= 3
        consts = [jnp.asarray(t) for t in tables(ey, ez, comps)]
        ahead, behind, z_ahead, z_rim, z_behind, lam_xy, lam_z = consts
        many = ey * comps
        vmem = pl.BlockSpec(memory_space=pltpu.VMEM)
        smem = pl.BlockSpec(memory_space=pltpu.SMEM)

        def shape(*dims):
            return pltpu.VMEM(dims, f32)

        def call(kernel, outs, args, scratch=(), smems=0, name=None):
            args = args[:smems] + [
                pltpu.with_memory_space_constraint(a, pltpu.VMEM) for a in args[smems:]
            ]
            return pl.pallas_call(
                kernel,
                out_shape=outs,
                in_specs=[smem] * smems + [vmem] * (len(args) - smems),
                out_specs=[vmem] * len(outs),
                scratch_shapes=list(scratch),
                name=name,
                compiler_params=pltpu.CompilerParams(vmem_limit_bytes=24 << 20),
            )(*args)

        def side_shapes(fields, more):
            return (
                [shape(fields * ny + more, nz)] * tx
                + [shape(fields * nx + more, nz)] * ty
                + [shape(8, nz)] * (tx * ty)
            )

        def send(arrays):
            out = []
            for a, pairs in zip(arrays, px + py + pxy):
                out.append(lax.ppermute(a, AXES, pairs))
            return out

        def received(at, refs, fields, with_extra):
            xs = both_sides(at[0], sizes[0], [r[...] for r in refs[:tx]])
            ys = both_sides(at[1], sizes[1], [r[...] for r in refs[tx : tx + ty]])
            if tx and ty:
                cs = four_corners(at, sizes, [r[...] for r in refs[tx + ty :]], ty)
            else:
                cs = [[jnp.zeros((8, nz), f32)] * 2] * 2
            more = 8 if with_extra else 0
            xs = [v if v is not None else jnp.zeros((fields * ny + more, nz), f32) for v in xs]
            ys = [v if v is not None else jnp.zeros((fields * nx + more, nz), f32) for v in ys]
            return xs, ys, cs

        def pack_kernel(vis, field, *outs):
            at = here()
            rows = [lane_row(vis, f, ez, e, nz) for f in range(ey)]
            pack_sides(at, [(field, c) for c in range(comps)], outs, (tx, ty), rows)

        faces = call(
            pack_kernel, side_shapes(comps, 8), [viscous, rhs], smems=1, name="pack_faces"
        )
        faces = send(faces)

        def window_kernel(vis, field, *refs):
            at = here()
            sides, (win, cols_out, around, coef, columns) = refs[:-5], refs[-5:]
            xs, ys, cs = received(at, sides, comps, True)
            pick = lambda v, c, n: v[c * n : (c + 1) * n]
            for c in range(comps):
                for f in range(ey):
                    fill_window(
                        win,
                        f * comps + c,
                        f,
                        ey,
                        lambda x, f: field[c, x, f * e : (f + 1) * e, :],
                        lambda y: field[c, :, y, :],
                        pick(xs[0], c, ny),
                        pick(xs[1], c, ny),
                        pick(ys[0], c, nx),
                        pick(ys[1], c, nx),
                        [[cs[s][t][c : c + 1] for t in (0, 1)] for s in (0, 1)],
                    )
            own = [lane_row(vis, f, ez, e, nz) for f in range(ey)]
            vx = [[xs[s][comps * ny + f : comps * ny + f + 1] for f in range(ey)] for s in (0, 1)]
            vy = [ys[s][comps * nx : comps * nx + 1] for s in (0, 1)]
            vc = [[cs[s][t][comps : comps + 1] for t in (0, 1)] for s in (0, 1)]
            flat = vx[0] + vx[1] + vy + vc[0] + vc[1]
            for k, row in enumerate(flat):
                around[k : k + 1, :] = row
            wide = lambda row: jnp.broadcast_to(row, (e, nz))
            for f in range(ey):
                face = [jnp.concatenate([wide(v) for v in vx[s]], axis=0) for s in (0, 1)]
                fill_window(
                    coef,
                    f,
                    f,
                    ey,
                    lambda x, f: wide(own[f]),
                    lambda y: wide(own[y // e]),
                    face[0],
                    face[1],
                    wide(vy[0]),
                    wide(vy[1]),
                    vc,
                )
            entries = []
            for f in range(ey):
                entries += [(f * 8 + 2 * c, win, f * comps + c) for c in range(comps)]
                entries += [(f * 8 + 2 * comps, coef, f)]
            gather_columns(columns, entries)
            cols_out[...] = columns[...].T[: ey * 8]

        windows, columns, around = call(
            window_kernel,
            [shape(many, ROWS, nz), shape(ey * 8, PLANE), shape(16, nz)],
            [viscous, rhs] + faces,
            [pltpu.VMEM((ey, ROWS, nz), f32), pltpu.VMEM((PLANE, LANES), f32)],
            smems=1,
            name="windows",
        )

        def send_z(array):
            return [lax.ppermute(array, AXES, pairs) for pairs in pz]

        def forward_kernel(win, ahead, z_ahead, out, stacked, mixed):
            for k in range(many):
                for p, piece in enumerate(three(win[k])):
                    stacked[p * ROWS : (p + 1) * ROWS, k * nz : (k + 1) * nz] = piece
            mixed[...] = jnp.dot(ahead[...], stacked[...], preferred_element_type=f32)
            for k in range(many):
                wide = jnp.concatenate(three(mixed[:, k * nz : (k + 1) * nz]), axis=1)
                out[k] = jnp.dot(wide, z_ahead[...], preferred_element_type=f32)

        def forward(windows):
            return call(
                forward_kernel,
                [shape(many, ROWS, 2 * LANES)],
                [windows, ahead, z_ahead],
                [pltpu.VMEM((3 * ROWS, many * nz), bf16), pltpu.VMEM((ROWS, many * nz), f32)],
                name="forward",
            )[0]

        def finish(store, modes, rim, tabs, vis, rea, stacked_rim, stacked):
            ahead, behind, z_rim, z_behind, lam_xy, lam_z = tabs
            lane = lax.broadcasted_iota(jnp.int32, (ROWS, LANES), 1)
            turned = rim[...].T
            for p, piece in enumerate(three(turned[:ROWS])):
                stacked_rim[p * ROWS : (p + 1) * ROWS, :] = piece
            plane = jnp.dot(ahead[...], stacked_rim[...], preferred_element_type=f32)

            def beside(v, part):
                lead, rest = split(v)
                lead, rest = lead.astype(f32), rest.astype(f32)
                both = jnp.where(lane < part, lead, pltpu.roll(rest, part, axis=1))
                far = jnp.where(lane < 2 * part, both, pltpu.roll(lead, 2 * part, axis=1))
                return far.astype(bf16)

            plane = beside(plane, ey * 16)
            for f in range(ey):
                v = lane_row(vis, f, ez, WINDOW, 2 * LANES)
                r = lane_row(rea, f, ez, WINDOW, 2 * LANES, fill=1.0)
                scale = 1.0 / (v * (lam_xy[...] + lam_z[...]) + r)
                for c in range(comps):
                    k = f * comps + c
                    m = modes[k] + jnp.dot(plane, z_rim[k], preferred_element_type=f32)
                    m = m * scale
                    lead, rest = split(m[:, :LANES])
                    tail = beside(m[:, LANES:], 32)
                    wide = jnp.concatenate([lead, rest, lead, tail], axis=1)
                    back = jnp.dot(wide, z_behind[...], preferred_element_type=f32)
                    for p, piece in enumerate(three(back)):
                        stacked[p * ROWS : (p + 1) * ROWS, k * nz : (k + 1) * nz] = piece
            local = jnp.dot(behind[...], stacked[...], preferred_element_type=f32)
            for f in range(ey):
                for c in range(comps):
                    k = f * comps + c
                    for x in range(nx):
                        store(c, x, f, local[x * e : (x + 1) * e, k * nz : (k + 1) * nz])

        tabs = [ahead, behind, z_rim, z_behind, lam_xy, lam_z]
        finish_scratch = [
            pltpu.VMEM((LANES, PLANE), f32),
            pltpu.VMEM((3 * ROWS, LANES), bf16),
            pltpu.VMEM((3 * ROWS, many * nz), bf16),
        ]

        def z_sides(at, refs, rows):
            got = both_sides(at[2], sizes[2], [r[...] for r in refs])
            return [v if v is not None else jnp.zeros((rows, PLANE), f32) for v in got]

        def first_kernel(vis, rea, field, modes, *refs):
            at = here()
            zs, refs = refs[:tz], refs[tz:]
            tabs, refs = refs[:6], refs[6:]
            first, part = refs[:2]
            outs, (rim, stacked_rim, stacked) = refs[2:-3], refs[-3:]
            low, high = z_sides(at, zs, ey * 8)
            rim[...] = jnp.zeros((LANES, PLANE), f32)
            for f in range(ey):
                for c in range(comps):
                    to, src = f * 16 + 4 * c, f * 8 + 2 * c
                    rim[to : to + 1, :] = low[src : src + 1]
                    rim[to + 1 : to + 2, :] = high[src + 1 : src + 2]

            def store(c, x, f, rows):
                first[c, x, f * e : (f + 1) * e, :] = rows

            finish(store, modes, rim, tabs, vis, rea, stacked_rim, stacked)
            wide = lambda row: jnp.broadcast_to(row, (e, nz))
            v = jnp.concatenate([wide(lane_row(vis, f, ez, e, nz)) for f in range(ey)], axis=0)
            r = jnp.concatenate([wide(lane_row(rea, f, ez, e, nz)) for f in range(ey)], axis=0)
            row = lax.broadcasted_iota(jnp.int32, (ny, nz), 0)
            lane = lax.broadcasted_iota(jnp.int32, (ny, nz), 1)
            for c in range(comps):
                for x in range(nx):
                    u = first[c, x]
                    near = jnp.where(row > 0, pltpu.roll(u, 1, axis=0), 0.0)
                    near += jnp.where(row < ny - 1, pltpu.roll(u, ny - 1, axis=0), 0.0)
                    near += jnp.where(lane > 0, pltpu.roll(u, 1, axis=1), 0.0)
                    near += jnp.where(lane < nz - 1, pltpu.roll(u, nz - 1, axis=1), 0.0)
                    if x > 0:
                        near += first[c, x - 1]
                    if x < nx - 1:
                        near += first[c, x + 1]
                    part[c, x] = field[c, x] - (r * u + v * (6.0 * u - near))
            fields = [(first, c) for c in range(comps)] + [(part, c) for c in range(comps)]
            pack_sides(at, fields, outs, (tx, ty))

        def residual_kernel(vis, first, part, around, *refs):
            at = here()
            sides, (win, cols_out, whole, own, columns) = refs[:-5], refs[-5:]
            xs, ys, cs = received(at, sides, 2 * comps, False)
            row = lax.broadcasted_iota(jnp.int32, (ny, nz), 0)
            line = lax.broadcasted_iota(jnp.int32, (nx, nz), 0)
            wide = lambda r: jnp.broadcast_to(r, (e, nz))
            mine = [lane_row(vis, f, ez, e, nz) for f in range(ey)]
            v = jnp.concatenate([wide(m) for m in mine], axis=0)
            near = lambda k: around[k : k + 1, :]
            vx = [
                jnp.concatenate([wide(near(s * ey + f)) for f in range(ey)], axis=0)
                for s in (0, 1)
            ]
            vy = [near(2 * ey + s) for s in (0, 1)]
            vc = [[near(2 * ey + 2 + 2 * s + t) for t in (0, 1)] for s in (0, 1)]
            for c in range(comps):
                ux = [xs[s][c * ny : (c + 1) * ny] for s in (0, 1)]
                rx = [xs[s][(comps + c) * ny : (comps + c + 1) * ny] for s in (0, 1)]
                uy = [ys[s][c * nx : (c + 1) * nx] for s in (0, 1)]
                ry = [ys[s][(comps + c) * nx : (comps + c + 1) * nx] for s in (0, 1)]
                uc = [[cs[s][t][c : c + 1] for t in (0, 1)] for s in (0, 1)]
                rc = [[cs[s][t][comps + c : comps + c + 1] for t in (0, 1)] for s in (0, 1)]
                at_x = (0, nx - 1)
                at_y = (0, ny - 1)
                for x in range(nx):
                    value = part[c, x]
                    for s in (0, 1):
                        if x == at_x[s]:
                            value += v * ux[s]
                    whole[x] = value
                for s in (0, 1):
                    f = 0 if s == 0 else ey - 1
                    whole[:, at_y[s], :] = whole[:, at_y[s], :] + mine[f] * uy[s]
                face_x = []
                for s in (0, 1):
                    beyond = jnp.where(row == 0, uc[s][0], jnp.where(row == ny - 1, uc[s][1], 0.0))
                    face_x.append(rx[s] + vx[s] * (first[c, at_x[s]] + beyond))
                face_y = []
                for t in (0, 1):
                    beyond = jnp.where(
                        line == 0, uc[0][t], jnp.where(line == nx - 1, uc[1][t], 0.0)
                    )
                    face_y.append(ry[t] + vy[t] * (first[c, :, at_y[t], :] + beyond))
                corner = [
                    [
                        rc[s][t]
                        + vc[s][t]
                        * (
                            ux[s][at_y[t] : at_y[t] + 1]
                            + uy[t][at_x[s] : at_x[s] + 1]
                        )
                        for t in (0, 1)
                    ]
                    for s in (0, 1)
                ]
                for f in range(ey):
                    k = f * comps + c
                    fill_window(
                        win,
                        k,
                        f,
                        ey,
                        lambda x, f: whole[x, f * e : (f + 1) * e, :],
                        lambda y: whole[:, y, :],
                        face_x[0],
                        face_x[1],
                        face_y[0],
                        face_y[1],
                        corner,
                    )
                    fill_window(
                        own,
                        k,
                        f,
                        ey,
                        lambda x, f: first[c, x, f * e : (f + 1) * e, :],
                        lambda y: first[c, :, y, :],
                        ux[0],
                        ux[1],
                        uy[0],
                        uy[1],
                        uc,
                    )
            entries = []
            for f in range(ey):
                for c in range(comps):
                    k = f * comps + c
                    entries.append((f * 16 + 2 * c, own, k))
                    entries.append((f * 16 + 2 * (comps + c), win, k))
            gather_columns(columns, entries)
            cols_out[...] = columns[...].T[: ey * 16]

        def last_kernel(vis, rea, first, modes, mine, coef, *refs):
            at = here()
            coefs, zs, refs = refs[:tz], refs[tz : 2 * tz], refs[2 * tz :]
            tabs, (out, rim, stacked_rim, stacked) = refs[:6], refs[6:]
            low, high = z_sides(at, zs, ey * 16)
            vlow, vhigh = z_sides(at, coefs, ey * 8)
            rim[...] = jnp.zeros((LANES, PLANE), f32)
            for f in range(ey):
                cv = f * 8 + 2 * comps
                v_last, v_first = coef[cv : cv + 1, :], coef[cv + 1 : cv + 2, :]
                for c in range(comps):
                    to, u, r = f * 16 + 4 * c, f * 16 + 2 * c, f * 16 + 2 * (comps + c)
                    u_last, u_first = mine[u : u + 1, :], mine[u + 1 : u + 2, :]
                    rim[to : to + 1, :] = low[r : r + 1] + vlow[cv : cv + 1] * u_first
                    rim[to + 1 : to + 2, :] = (
                        high[r + 1 : r + 2] + vhigh[cv + 1 : cv + 2] * u_last
                    )
                    rim[to + 2 : to + 3, :] = v_first * low[u : u + 1]
                    rim[to + 3 : to + 4, :] = v_last * high[u + 1 : u + 2]

            def store(c, x, f, rows):
                here_rows = slice(f * e, (f + 1) * e)
                out[c, x, here_rows, :] = first[c, x, here_rows, :] + rows

            finish(store, modes, rim, tabs, vis, rea, stacked_rim, stacked)

        z_first = send_z(columns)
        modes = forward(windows)
        results = call(
            first_kernel,
            [shape(*rhs.shape), shape(*rhs.shape)] + side_shapes(2 * comps, 0),
            [viscous, reaction, rhs, modes] + z_first + tabs,
            finish_scratch,
            smems=2,
            name="first",
        )
        first, part = results[:2]
        faces = send(results[2:])
        windows, columns2 = call(
            residual_kernel,
            [shape(many, ROWS, nz), shape(ey * 16, PLANE)],
            [viscous, first, part, around] + faces,
            [
                pltpu.VMEM((nx, ny, nz), f32),
                pltpu.VMEM((many, ROWS, nz), f32),
                pltpu.VMEM((PLANE, LANES), f32),
            ],
            smems=1,
            name="residual",
        )
        z_second = send_z(columns2)
        modes = forward(windows)
        return call(
            last_kernel,
            [jax.ShapeDtypeStruct(rhs.shape, f32)],
            [viscous, reaction, first, modes, columns2, columns] + z_first + z_second + tabs,
            finish_scratch,
            smems=2,
            name="last",
        )[0]

    placed = (P(None, *AXES), P(*AXES), P(*AXES))
    return jax.shard_map(
        shards, mesh=mesh, in_specs=placed, out_specs=P(None, *AXES), check_vma=False
    )
```

```python
import itertools

import jax
import jax.numpy as jnp
import numpy as np
from jax import lax
from jax.experimental import pallas as pl
from jax.experimental.pallas import tpu as pltpu
from jax.sharding import PartitionSpec as P

EDGE_POINTS = 16
WINDOW = EDGE_POINTS + 2
LANES = 128
MAIN = 160
HALF = 176
ROWS = 2 * HALF
PLANE = 384
DEEP = 3 * MAIN + 16
AXES = ("gx", "gy", "gz")
f32, bf16 = jnp.float32, jnp.bfloat16


def pairings(n):
    if n == 1:
        return []
    even = [c ^ 1 if c ^ 1 < n else c for c in range(n)]
    if n == 2:
        return [even]
    odd = [(c + 1 if c % 2 else c - 1) for c in range(n)]
    odd = [t % n if n % 2 == 0 else (t if 0 <= t < n else c) for c, t in enumerate(odd)]
    return [even, odd]


def swap_pairs(sizes, maps):
    def linear(c):
        return (c[0] * sizes[1] + c[1]) * sizes[2] + c[2]

    return [
        (linear(c), linear(maps(c))) for c in itertools.product(*[range(k) for k in sizes])
    ]


def plan(sizes):
    tx, ty, tz = (pairings(k) for k in sizes)
    px = [swap_pairs(sizes, lambda c, t=t: (t[c[0]], c[1], c[2])) for t in tx]
    py = [swap_pairs(sizes, lambda c, t=t: (c[0], t[c[1]], c[2])) for t in ty]
    pxy = [
        swap_pairs(sizes, lambda c, t=t, s=s: (t[c[0]], s[c[1]], c[2])) for t in tx for s in ty
    ]
    pz = []
    for k, t in enumerate(tz):
        if k == 1 and sizes[2] % 2 == 0 and sizes[0] % 2 == 0:
            ends = (0, sizes[2] - 1)
            pz.append(
                swap_pairs(
                    sizes,
                    lambda c, t=t, ends=ends: (tx[0][c[0]], c[1], c[2])
                    if c[2] in ends
                    else (c[0], c[1], t[c[2]]),
                )
            )
        else:
            pz.append(swap_pairs(sizes, lambda c, t=t: (c[0], c[1], t[c[2]])))
    return px, py, pxy, pz


def window_order():
    inner = range(1, EDGE_POINTS + 1)
    half = range(1, EDGE_POINTS // 2 + 1)
    last = EDGE_POINTS + 1
    order = [(i, j) for i in half for j in inner] + [(0, j) for j in inner]
    return order + [(i, 0) for i in half] + [(i, last) for i in half] + [(0, 0), (0, last)]


def pieces(table):
    table = np.asarray(table, np.float32)
    lead = table.astype(jnp.bfloat16)
    return lead, (table - lead.astype(np.float32)).astype(jnp.bfloat16)


def stacked_table(table):
    lead, rest = pieces(table)
    out = np.zeros((table.shape[0], 512), jnp.bfloat16)
    for k, piece in enumerate((lead, lead, rest)):
        out[:, k * MAIN : (k + 1) * MAIN] = piece[:, :MAIN]
        out[:, 3 * MAIN + 2 * k : 3 * MAIN + 2 * k + 2] = piece[:, MAIN : MAIN + 2]
    return out


def tables(ey, ez, comps):
    index = np.arange(WINDOW)
    basis = np.sqrt(2.0 / (EDGE_POINTS + 3)) * np.sin(
        np.pi * (index[:, None] + 1.0) * (index[None, :] + 1.0) / (EDGE_POINTS + 3)
    )
    lam = 2.0 - 2.0 * np.cos(np.pi * (index + 1.0) / (EDGE_POINTS + 3))
    order = window_order()
    inner = basis[1 : EDGE_POINTS + 1]
    valid = WINDOW * WINDOW // 2
    nz, width = EDGE_POINTS * ez, WINDOW * ez
    blocks = []
    lam_all = np.ones((2 * HALF, 2 * LANES), np.float32)
    places = [(m, m) for m in range(width)] + [(m, m + 32) for m in range(LANES, width)]
    for s in (0, 1):
        forward = np.zeros((HALF, valid))
        for k, (i, j) in enumerate(order):
            forward[:valid, k] = np.outer(basis[i, s::2], basis[j]).reshape(-1)
        blocks.append(stacked_table(forward))
        lam_xy = (lam[s::2, None] + lam[None, :]).reshape(-1)
        for m, lane in places:
            lam_all[s * HALF : s * HALF + valid, lane] = lam_xy + lam[m % WINDOW]
    for s in (0, 1):
        back = np.kron(inner[: EDGE_POINTS // 2, s::2], inner)
        blocks.append(stacked_table(back))
    depth = np.zeros((nz + 2, 2 * LANES))
    depth_back = np.zeros((width, nz))
    for m, lane in places:
        h, g = divmod(m, WINDOW)
        depth[h * EDGE_POINTS : h * EDGE_POINTS + WINDOW, lane] = basis[:, g]
        depth_back[m, h * EDGE_POINTS : (h + 1) * EDGE_POINTS] = inner[:, g]
    zh, zl = pieces(depth)
    ih, il = pieces(depth_back)
    core = slice(1, nz + 1)
    blocks.append(np.concatenate([zh[core], zl[core]], axis=1))
    z_back = np.zeros((2 * LANES, 2 * LANES), jnp.bfloat16)
    z_back[:LANES] = np.concatenate([ih[:LANES], il[:LANES]], axis=1)
    rest = width - LANES
    z_back[LANES : LANES + rest] = np.concatenate([ih[LANES:], il[LANES:]], axis=1)
    z_back[LANES + 32 : LANES + 32 + rest, :nz] = ih[LANES:]
    twice = np.zeros((2 * LANES, 2 * LANES), jnp.bfloat16)
    twice[:LANES, :nz] = ih[:LANES]
    twice[LANES:, nz:] = ih[:LANES]
    blocks.append(np.concatenate([z_back, twice], axis=1))
    rim = [0, nz + 1, 1, nz]
    part = ey * 16
    many = ey * comps
    z_rim = np.zeros((many + many % 2, 3 * part, 2 * LANES), jnp.bfloat16)
    for f in range(ey):
        for c in range(comps):
            for r, row in enumerate(rim):
                lane = f * 16 + 4 * c + r
                z_rim[f * comps + c, lane] = zh[row]
                z_rim[f * comps + c, part + lane] = zh[row]
                z_rim[f * comps + c, 2 * part + lane] = zl[row]
    for k in range(0, many, 2):
        blocks.append(np.concatenate([z_rim[k], z_rim[k + 1]], axis=1))
    at = np.cumsum([0] + [len(b) for b in blocks])
    return np.concatenate(blocks, axis=0), [int(v) for v in at], lam_all


def split(v):
    lead = v.astype(bf16)
    return lead, (v - lead.astype(f32)).astype(bf16)


def stack(v, out, at):
    lanes = slice(at, at + v.shape[1])
    lead, rest = split(v[:MAIN])
    for k, piece in enumerate((lead, rest, lead)):
        out[k * MAIN : (k + 1) * MAIN, lanes] = piece
    last = v[MAIN:]
    top = last.astype(bf16).astype(f32)
    ends = top + pltpu.roll(last - top, 2, axis=0) + pltpu.roll(top, 4, axis=0)
    out[3 * MAIN :, lanes] = ends.astype(bf16)


def both_sides(position, count, arrays):
    if not arrays:
        return None, None
    if len(arrays) == 1:
        low = high = arrays[0]
    else:
        odd = position % 2 == 1
        low = jnp.where(odd, arrays[0], arrays[1])
        high = jnp.where(odd, arrays[1], arrays[0])
    return (
        jnp.where(position > 0, low, jnp.zeros_like(low)),
        jnp.where(position < count - 1, high, jnp.zeros_like(high)),
    )


def four_corners(at, sizes, arrays, ny_types):
    rows = [arrays[k : k + ny_types] for k in range(0, len(arrays), ny_types)]
    by_y = [both_sides(at[0], sizes[0], [r[t] for r in rows]) for t in range(ny_types)]
    return [both_sides(at[1], sizes[1], [b[side] for b in by_y]) for side in (0, 1)]


def lane_row(ref, f, ez, step, width, fill=0.0):
    lane = lax.broadcasted_iota(jnp.int32, (1, width), 1)
    if width > LANES:
        lane = jnp.where(lane < LANES + 32, lane, lane - 32)
    row = jnp.full((1, width), fill, f32)
    for h in range(ez):
        value = jnp.broadcast_to(ref[0, f : f + 1, h : h + 1], (1, width))
        row = jnp.where((lane >= h * step) & (lane < (h + 1) * step), value, row)
    return row


def ends(position, kind, first, last):
    even = position % 2 == (1 if kind else 0)
    return jnp.where(even, last, first)


def slot_of(x, nx):
    return x if x < nx // 2 else nx // 2 + nx - 1 - x


def fill_window(out, k, f, ey, core, strip, xb, xa, yb, ya, corner):
    e = EDGE_POINTS
    h = e // 2
    for s, face in enumerate((xb, xa)):
        at = s * HALF
        for i in range(h):
            out[k, at + i * e : at + (i + 1) * e, :] = core(s * h + i, f)
        at += h * e
        out[k, at : at + e, :] = face[f * e : (f + 1) * e]
        at += e
        out[k, at : at + h, :] = (yb if f == 0 else strip(f * e - 1))[s]
        at += h
        out[k, at : at + h, :] = (ya if f == ey - 1 else strip((f + 1) * e))[s]
        at += h
        out[k, at : at + e, :] = jnp.zeros((e, LANES), f32)
        low = corner[s][0] if f == 0 else face[f * e - 1 : f * e]
        high = corner[s][1] if f == ey - 1 else face[(f + 1) * e : (f + 1) * e + 1]
        out[k, at : at + 1, :] = low
        out[k, at + 1 : at + 2, :] = high


def gather_columns(columns, refs):
    lane = lax.broadcasted_iota(jnp.int32, (ROWS, LANES), 1)
    total = jnp.zeros((ROWS, LANES), f32)
    for to, ref, k in refs:
        turned = pltpu.roll(ref[k], to + 1, axis=1)
        total = jnp.where((lane == to) | (lane == to + 1), turned, total)
    columns[0:ROWS, :] = total
    columns[ROWS:PLANE, :] = jnp.zeros((PLANE - ROWS, LANES), f32)


def solution(mesh):
    sizes = tuple(mesh.shape[a] for a in AXES)
    px, py, pxy, pz = plan(sizes)
    tx, ty, tz = len(px), len(py), len(pz)

    def here():
        return [lax.axis_index(a) for a in AXES]

    def shards(rhs, viscous, reaction):
        comps, nx, ny, nz = rhs.shape
        ex, ey, ez = viscous.shape
        e, h = EDGE_POINTS, EDGE_POINTS // 2
        assert ex == 1 and nz == LANES and WINDOW * ez <= 160 and ey * 48 <= LANES and comps <= 3
        field_in = rhs.reshape(comps, nx * ny, nz)
        table, at_row, lam = tables(ey, ez, comps)
        table, lam = jnp.asarray(table), jnp.asarray(lam)
        many = ey * comps
        vmem = pl.BlockSpec(memory_space=pltpu.VMEM)
        whole_shape = (comps, nx * ny, nz)
        slots = [slot_of(x, nx) for x in range(nx)]
        layer = [slots.index(j) for j in range(nx)]
        at_x, at_y = (0, nx - 1), (0, ny - 1)
        side_slot = (0, nx // 2)

        def shape(*dims, dtype=f32):
            return pltpu.VMEM(dims, dtype)

        def call(kernel, outs, args, scratch=(), name=None, free=()):
            spaces = [pltpu.HBM if k in free else pltpu.VMEM for k in range(len(args))]
            specs = [pl.BlockSpec(memory_space=space) for space in spaces]
            args = [
                pltpu.with_memory_space_constraint(a, space) for a, space in zip(args, spaces)
            ]
            return pl.pallas_call(
                kernel,
                out_shape=outs,
                in_specs=specs,
                out_specs=[vmem] * len(outs),
                scratch_shapes=list(scratch),
                name=name,
                compiler_params=pltpu.CompilerParams(vmem_limit_bytes=24 << 20),
            )(*args)

        def side_shapes(fields, more):
            return (
                [shape(fields * ny + more, nz)] * tx
                + [shape(fields * nx + more, nz)] * ty
                + [shape(8, nz)] * (tx * ty)
            )

        def send(arrays):
            return [lax.ppermute(a, AXES, pairs) for a, pairs in zip(arrays, px + py + pxy)]

        def send_z(arrays):
            return [lax.ppermute(a, AXES, pairs) for a, pairs in zip(arrays, pz)]

        def received(at, refs, fields, more):
            xs = both_sides(at[0], sizes[0], [r[...] for r in refs[:tx]])
            ys = both_sides(at[1], sizes[1], [r[...] for r in refs[tx : tx + ty]])
            if tx and ty:
                cs = four_corners(at, sizes, [r[...] for r in refs[tx + ty :]], ty)
            else:
                cs = [[jnp.zeros((8, nz), f32)] * 2] * 2
            xs = [v if v is not None else jnp.zeros((fields * ny + more, nz), f32) for v in xs]
            ys = [v if v is not None else jnp.zeros((fields * nx + more, nz), f32) for v in ys]
            return xs, ys, cs

        def halves(v):
            return v[:h], v[h:]

        def corner_rows(at, x_outs, xy_outs, total, extra):
            for k in range(tx):
                for s in range(ty):
                    for m in range(total):
                        low = x_outs[k][m * ny : m * ny + 1, :]
                        high = x_outs[k][(m + 1) * ny - 1 : (m + 1) * ny, :]
                        xy_outs[k * ty + s][m : m + 1, :] = ends(at[1], s, low, high)
                    if extra:
                        xy_outs[k * ty + s][total : total + 1, :] = ends(
                            at[1], s, extra[0], extra[-1]
                        )

        def pack_kernel(vis_in, field, *refs):
            at = here()
            outs, (vis, octets, sems) = refs[:-3], refs[-3:]
            x_outs, y_outs, xy_outs = outs[:tx], outs[tx : tx + ty], outs[tx + ty :]
            copies = [(vis_in, vis)]
            for t in range(2 if ty else 0):
                copies.append((field.at[:, :, t * (ny - 8) : t * (ny - 8) + 8, :], octets.at[t]))
            for k in range(tx):
                x = ends(at[0], k, 0, nx - 1)
                for c in range(comps):
                    copies.append((field.at[c, x], x_outs[k].at[c * ny : (c + 1) * ny]))
            copies = [
                pltpu.make_async_copy(src, dst, sems.at[k]) for k, (src, dst) in enumerate(copies)
            ]
            for copy in copies:
                copy.start()
            for copy in copies:
                copy.wait()
            extra = [lane_row(vis, f, ez, e, nz) for f in range(ey)]
            for k in range(tx):
                for f in range(ey):
                    x_outs[k][comps * ny + f : comps * ny + f + 1, :] = extra[f]
            for k in range(ty):
                for c in range(comps):
                    for x in range(nx):
                        row = ends(at[1], k, octets[0, c, x, 0:1, :], octets[1, c, x, 7:8, :])
                        to = c * nx + slots[x]
                        y_outs[k][to : to + 1, :] = row
                y_outs[k][comps * nx : comps * nx + 1, :] = ends(at[1], k, extra[0], extra[-1])
            corner_rows(at, x_outs, xy_outs, comps, extra)

        n_copies = 1 + comps * tx + (2 if ty else 0)
        faces = call(
            pack_kernel,
            side_shapes(comps, 8),
            [viscous, rhs],
            [
                pltpu.VMEM(viscous.shape, f32),
                pltpu.VMEM((2, comps, nx, 8, nz), f32),
                pltpu.SemaphoreType.DMA((n_copies,)),
            ],
            name="pack_faces",
            free=(0, 1),
        )

        def load_kernel(vis_in, rea_in, field, lam_in, after, own, rows, scale, *scratch):
            vis, rea, lam, sems = scratch
            copies = [(vis_in, vis), (rea_in, rea), (lam_in, lam), (field, own)]
            copies = [
                pltpu.make_async_copy(src, dst, sems.at[k]) for k, (src, dst) in enumerate(copies)
            ]
            for copy in copies:
                copy.start()
            for copy in copies[:3]:
                copy.wait()
            rows[...] = jnp.zeros((8, nz), f32)
            for f in range(ey):
                rows[f : f + 1, :] = lane_row(vis, f, ez, e, nz)
                rows[ey + f : ey + f + 1, :] = lane_row(rea, f, ez, e, nz)
                v = lane_row(vis, f, ez, WINDOW, 2 * LANES)
                r = lane_row(rea, f, ez, WINDOW, 2 * LANES, fill=1.0)
                scale[f] = 1.0 / (v * lam[...] + r)
            copies[3].wait()

        field_in, rows_in, scale_in = call(
            load_kernel,
            [shape(*whole_shape), shape(8, nz), shape(ey, ROWS, 2 * LANES)],
            [viscous, reaction, field_in, lam, faces[-1]],
            [
                pltpu.VMEM(viscous.shape, f32),
                pltpu.VMEM(viscous.shape, f32),
                pltpu.VMEM(lam.shape, f32),
                pltpu.SemaphoreType.DMA((4,)),
            ],
            name="load",
            free=(0, 1, 2, 3),
        )
        faces = send(faces)

        def spread_columns(columns, cols_out, tiles, pay, z):
            count = cols_out.shape[0]
            turned = columns[...].T[:count]
            cols_out[...] = turned
            for t in range(PLANE // LANES):
                some = slice(t * LANES, (t + 1) * LANES)
                tiles[t] = turned[:, some]
                last = tiles[t, pl.ds(0, count // 2, stride=2), :]
                first = tiles[t, pl.ds(1, count // 2, stride=2), :]
                for k in range(tz):
                    pay[k][:, some] = ends(z, k, first, last)

        def window_kernel(rows, field, *refs):
            at = here()
            split_at = len(refs) - 7 - tz
            sides, (win, cols_out, around, *refs) = refs[:split_at], refs[split_at:]
            pay, (coef, columns, turned, tiles) = refs[:tz], refs[tz:]
            xs, ys, cs = received(at, sides, comps, 8)
            pick = lambda v, c, n: v[c * n : (c + 1) * n]

            def strip(c, y):
                k = c * ey * 2 + (y // h) % (2 * ey)
                for i in range(h):
                    row = layer[h + i] * ny + y
                    turned[k, i : i + 1, :] = field[c, row : row + 1, :]
                return field[c, pl.ds(y, h, stride=ny), :], turned[k]

            for c in range(comps):
                for f in range(ey):
                    fill_window(
                        win,
                        f * comps + c,
                        f,
                        ey,
                        lambda j, f: field[c, layer[j] * ny + f * e : layer[j] * ny + (f + 1) * e, :],
                        lambda y: strip(c, y),
                        pick(xs[0], c, ny),
                        pick(xs[1], c, ny),
                        halves(pick(ys[0], c, nx)),
                        halves(pick(ys[1], c, nx)),
                        [[cs[s][t][c : c + 1] for t in (0, 1)] for s in (0, 1)],
                    )
            own = [rows[f : f + 1, :] for f in range(ey)]
            vx = [[xs[s][comps * ny + f : comps * ny + f + 1] for f in range(ey)] for s in (0, 1)]
            vy = [ys[s][comps * nx : comps * nx + 1] for s in (0, 1)]
            vc = [[cs[s][t][comps : comps + 1] for t in (0, 1)] for s in (0, 1)]
            flat = vx[0] + vx[1] + vy + vc[0] + vc[1]
            for k, row in enumerate(flat):
                around[k : k + 1, :] = row
            wide = lambda row: jnp.broadcast_to(row, (e, nz))
            for f in range(ey):
                face = [jnp.concatenate([wide(v) for v in vx[s]], axis=0) for s in (0, 1)]
                fill_window(
                    coef,
                    f,
                    f,
                    ey,
                    lambda j, f: wide(own[f]),
                    lambda y: halves(wide(own[y // e])),
                    face[0],
                    face[1],
                    halves(wide(vy[0])),
                    halves(wide(vy[1])),
                    vc,
                )
            entries = []
            for f in range(ey):
                entries += [(f * 8 + 2 * c, win, f * comps + c) for c in range(comps)]
                entries += [(f * 8 + 2 * comps, coef, f)]
            gather_columns(columns, entries)
            spread_columns(columns, cols_out, tiles, pay, at[2])

        windows, columns, around, *pay = call(
            window_kernel,
            [shape(many, ROWS, nz), shape(ey * 8, PLANE), shape(16, nz)]
            + [shape(ey * 4, PLANE)] * tz,
            [rows_in, field_in] + faces,
            [
                pltpu.VMEM((ey, ROWS, nz), f32),
                pltpu.VMEM((PLANE, LANES), f32),
                pltpu.VMEM((comps * ey * 2, h, nz), f32),
                pltpu.VMEM((PLANE // LANES, ey * 8, LANES), f32),
            ],
            name="windows",
        )

        def part_of(tab, k, rows=None, lanes=slice(None)):
            return tab[at_row[k] : at_row[k] + rows if rows else at_row[k + 1], lanes]

        def forward_kernel(win, tab, out, leads, *stacked):
            for k in range(many):
                low, high = win[k, :HALF], win[k, HALF:]
                stack(low + high, stacked[0], k * nz)
                stack(low - high, stacked[1], k * nz)
            z_lead = part_of(tab, 4, lanes=slice(0, 2 * LANES))
            z_twice = jnp.concatenate([z_lead, z_lead], axis=0)
            mixed = [
                jnp.dot(part_of(tab, s, lanes=slice(0, DEEP)), stacked[s][...], preferred_element_type=f32)
                for s in (0, 1)
            ]
            for k in range(many):
                both = [m[:, k * nz : (k + 1) * nz] for m in mixed]
                lead, rest = split(jnp.concatenate(both, axis=0))
                leads[k] = lead
                out[k] = jnp.dot(
                    jnp.concatenate([lead, rest], axis=1), z_twice, preferred_element_type=f32
                )

        def forward(windows):
            return call(
                forward_kernel,
                [shape(many, ROWS, 2 * LANES), shape(many, ROWS, LANES, dtype=bf16)],
                [windows, table],
                [pltpu.VMEM((DEEP, many * nz), bf16)] * 2,
                name="forward",
            )

        def finish(store, modes, leads, rim, tab, scale, stacked_rim, stacked):
            lane = lax.broadcasted_iota(jnp.int32, (ROWS, LANES), 1)
            part = ey * 16
            rows = rim[...]
            rest_rows = jnp.zeros((LANES - 3 * part, PLANE), f32)
            turned = jnp.concatenate([rows, rows, rows, rest_rows], axis=0).T
            low, high = turned[:HALF], turned[HALF : 2 * HALF]
            stack(low + high, stacked_rim[0], 0)
            stack(low - high, stacked_rim[1], 0)
            plane = jnp.concatenate(
                [
                    jnp.dot(
                        part_of(tab, s, lanes=slice(0, DEEP)),
                        stacked_rim[s][...],
                        preferred_element_type=f32,
                    )
                    for s in (0, 1)
                ],
                axis=0,
            )
            lead = plane.astype(bf16).astype(f32)
            middle = (lane >= part) & (lane < 2 * part)
            plane = jnp.where(middle, plane - lead, lead).astype(bf16)[:, : 3 * part]
            z_rest = part_of(tab, 4, lanes=slice(2 * LANES, 4 * LANES))
            z_back = part_of(tab, 5, lanes=slice(0, 2 * LANES))
            z_pair = part_of(tab, 5, lanes=slice(2 * LANES, 4 * LANES))
            for f in range(ey):
                for c in range(comps):
                    k = f * comps + c
                    to = k % 2 * 2 * LANES
                    z_rim = part_of(tab, 6 + k // 2, lanes=slice(to, to + 2 * LANES))
                    m = modes[k] + jnp.dot(
                        jnp.concatenate([leads[k], plane], axis=1),
                        jnp.concatenate([z_rest, z_rim], axis=0),
                        preferred_element_type=f32,
                    )
                    m = m * scale[f]
                    lead, rest = split(m[:, :LANES])
                    over = m[:, LANES:]
                    top = over.astype(bf16).astype(f32)
                    over = jnp.where(lane < 32, top, over - top).astype(bf16)
                    a = jnp.dot(
                        jnp.concatenate([lead, over], axis=1), z_back, preferred_element_type=f32
                    )
                    b = jnp.dot(
                        jnp.concatenate([rest[:HALF], rest[HALF:]], axis=1),
                        z_pair,
                        preferred_element_type=f32,
                    )
                    for s in (0, 1):
                        mine = a[s * HALF : (s + 1) * HALF]
                        back = mine[:, :nz] + mine[:, nz:] + b[:, s * nz : (s + 1) * nz]
                        stack(back, stacked[s], k * nz)
            local = [
                jnp.dot(
                    part_of(tab, 2 + s, lanes=slice(0, DEEP)),
                    stacked[s][...],
                    preferred_element_type=f32,
                )
                for s in (0, 1)
            ]
            for f in range(ey):
                for c in range(comps):
                    k = f * comps + c
                    for i in range(h):
                        even, odd = [
                            m[i * e : (i + 1) * e, k * nz : (k + 1) * nz] for m in local
                        ]
                        store(c, i, f, even + odd)
                        store(c, h + i, f, even - odd)

        finish_scratch = (
            [pltpu.VMEM((ey * 16, PLANE), f32)]
            + [pltpu.VMEM((DEEP, LANES), bf16)] * 2
            + [pltpu.VMEM((DEEP, many * nz), bf16)] * 2
        )

        def z_sides(at, refs, rows):
            got = both_sides(at[2], sizes[2], [r[...] for r in refs])
            return [v if v is not None else jnp.zeros((rows, PLANE), f32) for v in got]

        def first_kernel(rows, field, modes, leads, tab, scale, *refs):
            at = here()
            zs, (first, part) = refs[:tz], refs[tz : tz + 2]
            outs, (rim, *stacks) = refs[tz + 2 : -5], refs[-5:]
            low, high = z_sides(at, zs, ey * 4)
            rim[...] = jnp.zeros((ey * 16, PLANE), f32)
            for f in range(ey):
                for c in range(comps):
                    to, src = f * 16 + 4 * c, f * 4 + c
                    rim[to : to + 1, :] = low[src : src + 1]
                    rim[to + 1 : to + 2, :] = high[src : src + 1]

            def store(c, j, f, value):
                first[c, j * ny + f * e : j * ny + (f + 1) * e, :] = value

            finish(store, modes, leads, rim, tab, scale, stacks[:2], stacks[2:])
            wide = lambda row: jnp.broadcast_to(row, (e, nz))
            v = jnp.concatenate([wide(rows[f : f + 1, :]) for f in range(ey)], axis=0)
            r = jnp.concatenate([wide(rows[ey + f : ey + f + 1, :]) for f in range(ey)], axis=0)
            main = r + 6.0 * v
            row = lax.broadcasted_iota(jnp.int32, (ny, nz), 0)
            lane = lax.broadcasted_iota(jnp.int32, (ny, nz), 1)
            take = lambda c, x: first[c, slots[x] * ny : (slots[x] + 1) * ny, :]
            for c in range(comps):
                for x in range(nx):
                    u = take(c, x)
                    near = jnp.where(row > 0, pltpu.roll(u, 1, axis=0), 0.0)
                    near += jnp.where(row < ny - 1, pltpu.roll(u, ny - 1, axis=0), 0.0)
                    near += jnp.where(lane > 0, pltpu.roll(u, 1, axis=1), 0.0)
                    near += jnp.where(lane < nz - 1, pltpu.roll(u, nz - 1, axis=1), 0.0)
                    if x > 0:
                        near += take(c, x - 1)
                    if x < nx - 1:
                        near += take(c, x + 1)
                    part[c, slots[x] * ny : (slots[x] + 1) * ny, :] = (
                        field[c, x * ny : (x + 1) * ny, :] - main * u + v * near
                    )
            x_outs, y_outs, xy_outs = outs[:tx], outs[tx : tx + ty], outs[tx + ty :]
            for g, source in enumerate((first, part)):
                for c in range(comps):
                    m = g * comps + c
                    low, high = [source[c, j * ny : (j + 1) * ny, :] for j in side_slot]
                    for k in range(tx):
                        x_outs[k][m * ny : (m + 1) * ny, :] = ends(at[0], k, low, high)
                    if ty:
                        low, high = [source[c, pl.ds(y, nx, stride=ny), :] for y in at_y]
                    for k in range(ty):
                        y_outs[k][m * nx : (m + 1) * nx, :] = ends(at[1], k, low, high)
            corner_rows(at, x_outs, xy_outs, 2 * comps, None)

        def residual_kernel(rows, first, part, around, *refs):
            at = here()
            split_at = len(refs) - 6 - tz
            sides, (win, cols_out, *refs) = refs[:split_at], refs[split_at:]
            pay, (whole, own, columns, tiles) = refs[:tz], refs[tz:]
            xs, ys, cs = received(at, sides, 2 * comps, 0)
            row = lax.broadcasted_iota(jnp.int32, (ny, nz), 0)
            line = lax.broadcasted_iota(jnp.int32, (nx, nz), 0)
            wide = lambda r: jnp.broadcast_to(r, (e, nz))
            mine = [rows[f : f + 1, :] for f in range(ey)]
            v = jnp.concatenate([wide(m) for m in mine], axis=0)
            near = lambda k: around[k : k + 1, :]
            vx = [
                jnp.concatenate([wide(near(s * ey + f)) for f in range(ey)], axis=0)
                for s in (0, 1)
            ]
            vy = [near(2 * ey + s) for s in (0, 1)]
            vc = [[near(2 * ey + 2 + 2 * s + t) for t in (0, 1)] for s in (0, 1)]
            for c in range(comps):
                ux = [xs[s][c * ny : (c + 1) * ny] for s in (0, 1)]
                rx = [xs[s][(comps + c) * ny : (comps + c + 1) * ny] for s in (0, 1)]
                uy = [ys[s][c * nx : (c + 1) * nx] for s in (0, 1)]
                ry = [ys[s][(comps + c) * nx : (comps + c + 1) * nx] for s in (0, 1)]
                uc = [[cs[s][t][c : c + 1] for t in (0, 1)] for s in (0, 1)]
                rc = [[cs[s][t][comps + c : comps + c + 1] for t in (0, 1)] for s in (0, 1)]
                layer_rows = lambda j: slice(j * ny, (j + 1) * ny)
                for j in range(nx):
                    value = part[c, layer_rows(j), :]
                    for s in (0, 1):
                        if j == side_slot[s]:
                            value += v * ux[s]
                    whole[c, layer_rows(j), :] = value
                for s in (0, 1):
                    f = 0 if s == 0 else ey - 1
                    line_of = pl.ds(at_y[s], nx, stride=ny)
                    whole[c, line_of, :] = whole[c, line_of, :] + mine[f] * uy[s]
                face_x = []
                for s in (0, 1):
                    beyond = jnp.where(row == 0, uc[s][0], jnp.where(row == ny - 1, uc[s][1], 0.0))
                    face_x.append(rx[s] + vx[s] * (first[c, layer_rows(side_slot[s]), :] + beyond))
                face_y = []
                for t in (0, 1):
                    beyond = jnp.where(
                        line == side_slot[0],
                        uc[0][t],
                        jnp.where(line == side_slot[1], uc[1][t], 0.0),
                    )
                    line_of = pl.ds(at_y[t], nx, stride=ny)
                    face_y.append(ry[t] + vy[t] * (first[c, line_of, :] + beyond))
                corner = [
                    [
                        rc[s][t]
                        + vc[s][t]
                        * (
                            ux[s][at_y[t] : at_y[t] + 1]
                            + uy[t][side_slot[s] : side_slot[s] + 1]
                        )
                        for t in (0, 1)
                    ]
                    for s in (0, 1)
                ]
                for f in range(ey):
                    k = f * comps + c
                    for out, source, fx, fy, cor in (
                        (win, whole, face_x, face_y, corner),
                        (own, first, ux, uy, uc),
                    ):
                        fill_window(
                            out,
                            k,
                            f,
                            ey,
                            lambda j, f: source[c, j * ny + f * e : j * ny + (f + 1) * e, :],
                            lambda y: halves(source[c, pl.ds(y, nx, stride=ny), :]),
                            fx[0],
                            fx[1],
                            halves(fy[0]),
                            halves(fy[1]),
                            cor,
                        )
            entries = []
            for f in range(ey):
                for c in range(comps):
                    k = f * comps + c
                    entries.append((f * 16 + 2 * c, own, k))
                    entries.append((f * 16 + 2 * (comps + c), win, k))
            gather_columns(columns, entries)
            spread_columns(columns, cols_out, tiles, pay, at[2])

        def last_kernel(first, modes, leads, tab, scale, mine, coef, *refs):
            at = here()
            coefs, zs, (out, rim, *stacks) = refs[:tz], refs[tz : 2 * tz], refs[2 * tz :]
            low, high = z_sides(at, zs, ey * 8)
            vlow, vhigh = z_sides(at, coefs, ey * 4)
            rim[...] = jnp.zeros((ey * 16, PLANE), f32)
            for f in range(ey):
                cv = f * 8 + 2 * comps
                v_last, v_first = coef[cv : cv + 1, :], coef[cv + 1 : cv + 2, :]
                for c in range(comps):
                    to, u = f * 16 + 4 * c, f * 16 + 2 * c
                    got, near = f * 8 + c, f * 4 + comps
                    u_last, u_first = mine[u : u + 1, :], mine[u + 1 : u + 2, :]
                    part = got + comps
                    rim[to : to + 1, :] = low[part : part + 1] + vlow[near : near + 1] * u_first
                    rim[to + 1 : to + 2, :] = (
                        high[part : part + 1] + vhigh[near : near + 1] * u_last
                    )
                    rim[to + 2 : to + 3, :] = v_first * low[got : got + 1]
                    rim[to + 3 : to + 4, :] = v_last * high[got : got + 1]

            def store(c, j, f, rows):
                x = layer[j]
                out[c, x * ny + f * e : x * ny + (f + 1) * e, :] = (
                    first[c, j * ny + f * e : j * ny + (f + 1) * e, :] + rows
                )

            finish(store, modes, leads, rim, tab, scale, stacks[:2], stacks[2:])

        z_first = send_z(pay)
        modes = forward(windows)
        results = call(
            first_kernel,
            [shape(*whole_shape)] * 2 + side_shapes(2 * comps, 0),
            [rows_in, field_in] + list(modes) + [table, scale_in] + z_first,
            finish_scratch,
            name="first",
        )
        first, part = results[:2]
        faces = send(results[2:])
        windows, columns2, *pay = call(
            residual_kernel,
            [shape(many, ROWS, nz), shape(ey * 16, PLANE)] + [shape(ey * 8, PLANE)] * tz,
            [rows_in, first, part, around] + faces,
            [
                pltpu.VMEM(whole_shape, f32),
                pltpu.VMEM((many, ROWS, nz), f32),
                pltpu.VMEM((PLANE, LANES), f32),
                pltpu.VMEM((PLANE // LANES, ey * 16, LANES), f32),
            ],
            name="residual",
        )
        z_second = send_z(pay)
        modes = forward(windows)
        result = call(
            last_kernel,
            [jax.ShapeDtypeStruct(whole_shape, f32)],
            [first] + list(modes) + [table, scale_in, columns2, columns]
            + z_first
            + z_second,
            finish_scratch,
            name="last",
        )[0]
        return result.reshape(rhs.shape)

    placed = (P(None, *AXES), P(*AXES), P(*AXES))
    return jax.shard_map(
        shards, mesh=mesh, in_specs=placed, out_specs=P(None, *AXES), check_vma=False
    )
```
